32 devices in a mesh: row: 4 (over y, x), col: 8 (over z, core).
Axes of the slice: x: 2, y: 2, z: 4, core: 2. Of those that a mesh axis runs over, the one named last changes fastest.
Arguments:
- source_slab: float32 [2, 1024, 10240], P(None, 'row', 'col'), may hold values from -6 to 6
- receiver_side: float32 [2, 4096, 10240], P(None, 'col', 'row'), may hold values from -6 to 6
- surface_weight: float32 [2, 10240], P(None, 'row'), may hold values from -0.0390625 to 0.0390625
- recorded: float32 [2, 1024, 4096], P(None, 'row', 'col'), may hold values from -6 to 6
- matching_taps: float32 [41, 512], P(None, ('row', 'col')), may hold values from -1 to 1
- source_group: int32 [1024], P('row'), may hold values from 0 to 15, never falling along the last dimension, each value on 1 to 128 neighbouring positions
- receiver_window: int32 [4096], P('col'), may hold values from 0 to 31, never falling along the last dimension, each value on 1 to 256 neighbouring positions
Outputs:
- multiples: float32 [2, 1024, 4096], P(None, 'row', 'col')
- primaries: float32 [2, 1024, 4096], P(None, 'row', 'col')
The draws below stay inside these ranges and needn't reach their ends.
Inputs may be any that keep to these rules, and one draw needn't show every extreme that they name: `source_group`: never falls along the sources; each of the 16 groups holds 1 to 128 sources, one group exactly 128. `receiver_window`: never falls along the receivers; each of the 32 windows holds 1 to 256 receivers, one window exactly 256.
All inputs are finite; a program needn't handle non-finite values.
Results may differ from the reference program's by a relative error of at most 0.000071.
Values sent between devices are 32-bit elements; how exact they have to be, the bound alone decides.
No kernel may reach another device: no remote copies, remote signals or barrier semaphores. Data moves between devices by JAX's collectives and lax.ppermute only.
A program may use at most 192 MiB of HBM per device.

```python
import math
import jax
import jax.numpy as jnp
import numpy as np
from jax import lax

K = 10240
TAPS = 41
SOURCES = 1024
RECEIVERS = 4096
NGROUP = 16
NWIN = 32
NFILT = 512
SRC_MOST = 128
RCV_MOST = 256


def block_levels(own_key, extent, shards, least, largest):
    level = 1.0
    for dim, blocks in shards:
        steps = jax.random.uniform(jax.random.fold_in(jax.random.fold_in(own_key, 6), dim), (blocks,), jnp.float32, least / len(shards), largest / len(shards))
        level = level * jnp.repeat(jnp.exp(steps), extent[dim] // blocks).reshape((-1,) + (1,) * (len(extent) - 1 - dim))
    return level


def profile(number_of, total, bound, skew):
    portions = [(1 << 20) // math.isqrt(grade ** skew) + 1 for grade in range(2, number_of + 1)]
    spare, holding = total - bound - (number_of - 1), [1] * (number_of - 1)
    while spare > 0:
        movable = [i for i in range(number_of - 1) if holding[i] < bound]
        mass, left = sum([portions[i] for i in movable]), spare
        for i in movable:
            more = min(bound - holding[i], max(1, left * portions[i] // mass), spare)
            holding[i] = holding[i] + more
            spare = spare - more
    return np.array([bound] + holding)


def uneven(stream_key, count, total, bound, skew):
    if count == 2:
        one = jax.random.randint(stream_key, (), max(1, total - bound), min(bound, total - 1) + 1)
        return jnp.stack([one, total - one])
    sizes = jnp.asarray(profile(count, total, bound, skew), jnp.int32)
    twos = (count - 1) // 2
    source_of, receiver = sizes[1:1 + 2 * twos:2], sizes[2:2 + 2 * twos:2]
    margin = jnp.minimum(source_of - 1, bound - receiver)
    shifted = jax.random.randint(jax.random.fold_in(stream_key, 1), (twos,), 0, 1 << 20) % (margin + 1)
    sizes = sizes.at[1:1 + 2 * twos:2].set(source_of - shifted).at[2:2 + 2 * twos:2].set(receiver + shifted)
    return sizes[jax.random.permutation(jax.random.fold_in(stream_key, 2), count)]


def scatter_about(own_key, extent, width, limit, pieces=(), kind=jnp.bfloat16):
    factor_of = block_levels(own_key, extent, pieces, -0.22, 0.18) if pieces else 1.0
    result = jax.random.normal(own_key, extent, jnp.float32) * width * factor_of
    return jnp.minimum(jnp.maximum(result, -limit), limit).astype(kind)


def setup_inputs(seed: int = 0) -> dict:
    seeds = jax.random.split(jax.random.key(seed), 8)
    source_slab = scatter_about(seeds[0], (2, SOURCES, K), 1.0, 6.0, ((1, 4), (2, 8)), jnp.float32)
    receiver_side = scatter_about(seeds[1], (2, RECEIVERS, K), 1.0, 6.0, ((1, 8), (2, 4)), jnp.float32)
    surface_weight = scatter_about(seeds[2], (2, K), (2 * K) ** -0.5, 0.0390625, ((1, 4),), jnp.float32)
    recorded = scatter_about(seeds[3], (2, SOURCES, RECEIVERS), 1.0, 6.0, ((1, 4), (2, 8)), jnp.float32)
    matching_taps = scatter_about(seeds[4], (TAPS, NFILT), TAPS ** -0.5, 1.0, ((1, 32),), jnp.float32)
    source_group = jnp.searchsorted(jnp.cumsum(uneven(seeds[5], NGROUP, SOURCES, SRC_MOST, 1)), jnp.arange(SOURCES), side="right").astype(jnp.int32)
    receiver_window = jnp.searchsorted(jnp.cumsum(uneven(seeds[6], NWIN, RECEIVERS, RCV_MOST, 1)), jnp.arange(RECEIVERS), side="right").astype(jnp.int32)
    return dict(source_slab=source_slab, receiver_side=receiver_side, surface_weight=surface_weight, recorded=recorded, matching_taps=matching_taps, source_group=source_group, receiver_window=receiver_window)


PHASE_STEP = 0.37
PRECISE = lax.Precision.HIGHEST


def contract(left_side, right_side):
    return lax.dot_general(left_side, right_side, (((1,), (1,)), ((), ())), precision=PRECISE, preferred_element_type=jnp.float32)


def weighted(receiver_side, surface_weight):
    weight_real = receiver_side[0] * surface_weight[0][None, :] - receiver_side[1] * surface_weight[1][None, :]
    weight_imag = receiver_side[0] * surface_weight[1][None, :] + receiver_side[1] * surface_weight[0][None, :]
    return weight_real, weight_imag


def responses(matching_taps):
    center = (matching_taps.shape[0] - 1) / 2.0
    phases = PHASE_STEP * (jnp.arange(matching_taps.shape[0], dtype=jnp.float32) - center)
    phase_table = jnp.stack([jnp.cos(phases), -jnp.sin(phases)])
    return jnp.dot(phase_table, matching_taps, precision=PRECISE, preferred_element_type=jnp.float32)


def reference(source_slab, receiver_side, surface_weight, recorded, matching_taps, source_group, receiver_window):
    weight_real, weight_imag = weighted(receiver_side, surface_weight)
    multiple_real = contract(source_slab[0], weight_real) - contract(source_slab[1], weight_imag)
    multiple_imag = contract(source_slab[0], weight_imag) + contract(source_slab[1], weight_real)
    response = responses(matching_taps)
    filter_index = (receiver_window[None, :] * NGROUP + source_group[:, None]).astype(jnp.int32)
    applied_real = response[0][filter_index]
    applied_imag = response[1][filter_index]
    primary_real = recorded[0] - (applied_real * multiple_real - applied_imag * multiple_imag)
    primary_imag = recorded[1] - (applied_real * multiple_imag + applied_imag * multiple_real)
    multiples = jnp.stack([multiple_real, multiple_imag])
    primaries = jnp.stack([primary_real, primary_imag])
    return (multiples, primaries)
```

```python
import jax
import jax.numpy as jnp
from jax import lax
from jax.sharding import PartitionSpec as P

PHASE_STEP = 0.37
PRECISE = lax.Precision.HIGHEST
CHUNKS = 4
LANES = 2


def contract(left_side, right_side):
    return lax.dot_general(
        left_side,
        right_side,
        (((1,), (1,)), ((), ())),
        precision=lax.Precision.HIGH,
        preferred_element_type=jnp.float32,
    )


def weighted(receiver_side, surface_weight):
    weight_real = (
        receiver_side[0] * surface_weight[0][None, :]
        - receiver_side[1] * surface_weight[1][None, :]
    )
    weight_imag = (
        receiver_side[0] * surface_weight[1][None, :]
        + receiver_side[1] * surface_weight[0][None, :]
    )
    return (weight_real, weight_imag)


def responses(matching_taps):
    center = (matching_taps.shape[0] - 1) / 2.0
    phases = PHASE_STEP * (jnp.arange(matching_taps.shape[0], dtype=jnp.float32) - center)
    phase_table = jnp.stack([jnp.cos(phases), -jnp.sin(phases)])
    return jnp.dot(
        phase_table, matching_taps, precision=PRECISE, preferred_element_type=jnp.float32
    )


def applied_response(matching_taps, source_group, receiver_window, rows):
    response = responses(matching_taps)
    own = response.shape[1]
    cols = lax.axis_size("col")
    place = (lax.axis_index("row") * cols + lax.axis_index("col")) * own
    response = lax.dynamic_update_slice_in_dim(
        jnp.zeros((2, rows * cols * own), jnp.float32), response, place, axis=1
    )
    for axis, extent in (("col", cols), ("row", rows)):
        step = 1
        while step < extent:
            swap = [(i, i ^ step) for i in range(extent)]
            response = response + lax.ppermute(response, axis, swap)
            step *= 2
    groups = 4 * rows
    windows = response.shape[1] // groups
    response_grid = response.reshape(2, windows, groups)
    group_hot = (source_group[:, None] == jnp.arange(groups, dtype=jnp.int32)[None, :]).astype(
        jnp.float32
    )
    window_hot = (receiver_window[:, None] == jnp.arange(windows, dtype=jnp.int32)[None, :]).astype(
        jnp.float32
    )
    per_source = jnp.einsum("sg,cwg->csw", group_hot, response_grid, precision=PRECISE)
    return jnp.einsum("csw,rw->csr", per_source, window_hot, precision=PRECISE)


def pick(held, which):
    chosen = held[0]
    for number in range(1, len(held)):
        chosen = jnp.where(which == number, held[number], chosen)
    return chosen


def local(
    source_slab,
    receiver_side,
    surface_weight,
    recorded,
    matching_taps,
    source_group,
    receiver_window,
):
    rows, cols = lax.axis_size("row"), lax.axis_size("col")
    share = cols // rows
    row, col = lax.axis_index("row"), lax.axis_index("col")
    plane, part = col // share, col % share
    sources, depth = source_slab.shape[1], source_slab.shape[2]
    ring = [(c, (c - share) % cols) for c in range(cols)]
    across = [[(i, i ^ j) for i in range(rows)] for j in range(rows)]
    inner = [
        [(c, c // share * share + (c - q) % share) for c in range(cols)] for q in range(share)
    ]

    weight_real, weight_imag = weighted(receiver_side, surface_weight)
    sides = []
    for q in range(share):
        start = (part + q) % share * depth
        sides.append(
            (
                lax.dynamic_slice_in_dim(weight_real, start, depth, axis=1),
                lax.dynamic_slice_in_dim(weight_imag, start, depth, axis=1),
            )
        )
    mapped = applied_response(matching_taps, source_group, receiver_window, rows)

    size = sources // CHUNKS
    all_multiples, all_primaries = [], []
    ended = [None] * LANES
    for chunk in range(CHUNKS):
        span = slice(chunk * size, (chunk + 1) * size)
        held = [source_slab[:, span]]
        lane = chunk % LANES
        if ended[lane] is not None:
            held[0], _ = lax.optimization_barrier((held[0], ended[lane]))
        for _ in range(rows - 1):
            held.append(lax.ppermute(held[-1], "col", ring))
        ended[lane] = held[-1]
        blocks = []
        for j in range(rows):
            block = pick(held, ((row ^ j) - plane) % rows)
            blocks.append(block if j == 0 else lax.ppermute(block, "row", across[j]))
        mine = jnp.concatenate(blocks, axis=1)
        new_real, new_imag = 0.0, 0.0
        for q in range(share):
            portion = mine if q == 0 else lax.ppermute(mine, "col", inner[q])
            side_real, side_imag = sides[q]
            new_real += contract(portion[0], side_real) - contract(portion[1], side_imag)
            new_imag += contract(portion[0], side_imag) + contract(portion[1], side_real)
        partial = jnp.stack([new_real, new_imag])
        total = partial[:, :size]
        for j in range(1, rows):
            total += lax.ppermute(partial[:, j * size : (j + 1) * size], "row", across[j])
        here = mapped[:, span]
        primary_real = recorded[0, span] - (here[0] * total[0] - here[1] * total[1])
        primary_imag = recorded[1, span] - (here[0] * total[1] + here[1] * total[0])
        all_multiples.append(total)
        all_primaries.append(jnp.stack([primary_real, primary_imag]))
    return (jnp.concatenate(all_multiples, axis=1), jnp.concatenate(all_primaries, axis=1))


def solution(mesh):
    placed = (
        P(None, "row", "col"),
        P(None, "col", "row"),
        P(None, "row"),
        P(None, "row", "col"),
        P(None, ("row", "col")),
        P("row"),
        P("col"),
    )
    return jax.shard_map(
        local,
        mesh=mesh,
        in_specs=placed,
        out_specs=(P(None, "row", "col"), P(None, "row", "col")),
        check_vma=False,
    )
```

```python
import jax
import jax.numpy as jnp
from jax import lax
from jax.sharding import PartitionSpec as P

PHASE_STEP = 0.37
PRECISE = lax.Precision.HIGHEST
CHUNKS = 4
LANES = 2


def contract(left_side, right_side):
    return lax.dot_general(
        left_side,
        right_side,
        (((1,), (1,)), ((), ())),
        precision=lax.Precision.HIGH,
        preferred_element_type=jnp.float32,
    )


def weighted(receiver_side, surface_weight):
    weight_real = (
        receiver_side[0] * surface_weight[0][None, :]
        - receiver_side[1] * surface_weight[1][None, :]
    )
    weight_imag = (
        receiver_side[0] * surface_weight[1][None, :]
        + receiver_side[1] * surface_weight[0][None, :]
    )
    return (weight_real, weight_imag)


def responses(matching_taps):
    center = (matching_taps.shape[0] - 1) / 2.0
    phases = PHASE_STEP * (jnp.arange(matching_taps.shape[0], dtype=jnp.float32) - center)
    phase_table = jnp.stack([jnp.cos(phases), -jnp.sin(phases)])
    return jnp.dot(
        phase_table, matching_taps, precision=PRECISE, preferred_element_type=jnp.float32
    )


def applied_response(matching_taps, source_group, receiver_window, rows):
    response = responses(matching_taps)
    own = response.shape[1]
    cols = lax.axis_size("col")
    place = (lax.axis_index("row") * cols + lax.axis_index("col")) * own
    response = lax.dynamic_update_slice_in_dim(
        jnp.zeros((2, rows * cols * own), jnp.float32), response, place, axis=1
    )
    for axis, extent in (("col", cols), ("row", rows)):
        step = 1
        while step < extent:
            swap = [(i, i ^ step) for i in range(extent)]
            response = response + lax.ppermute(response, axis, swap)
            step *= 2
    groups = 4 * rows
    windows = response.shape[1] // groups
    response_grid = response.reshape(2, windows, groups)
    group_hot = (source_group[:, None] == jnp.arange(groups, dtype=jnp.int32)[None, :]).astype(
        jnp.float32
    )
    window_hot = (receiver_window[:, None] == jnp.arange(windows, dtype=jnp.int32)[None, :]).astype(
        jnp.float32
    )
    per_source = jnp.einsum("sg,cwg->csw", group_hot, response_grid, precision=PRECISE)
    return jnp.einsum("csw,rw->csr", per_source, window_hot, precision=PRECISE)


def pick(held, which):
    chosen = held[0]
    for number in range(1, len(held)):
        chosen = jnp.where(which == number, held[number], chosen)
    return chosen


def local(
    source_slab,
    receiver_side,
    surface_weight,
    recorded,
    matching_taps,
    source_group,
    receiver_window,
):
    rows, cols = lax.axis_size("row"), lax.axis_size("col")
    share = cols // rows
    row, col = lax.axis_index("row"), lax.axis_index("col")
    plane, part = col // share, col % share
    sources, depth = source_slab.shape[1], source_slab.shape[2]
    ring = [(c, (c - share) % cols) for c in range(cols)]
    across = [[(i, i ^ j) for i in range(rows)] for j in range(rows)]
    inner = [
        [(c, c // share * share + (c - q) % share) for c in range(cols)] for q in range(share)
    ]

    weight_real, weight_imag = weighted(receiver_side, surface_weight)
    sides = []
    for q in range(share):
        start = (part + q) % share * depth
        sides.append(
            (
                lax.dynamic_slice_in_dim(weight_real, start, depth, axis=1),
                lax.dynamic_slice_in_dim(weight_imag, start, depth, axis=1),
            )
        )
    mapped = applied_response(matching_taps, source_group, receiver_window, rows)

    size = sources // CHUNKS
    all_multiples, all_primaries = [], []
    ended = [None] * LANES
    partials, arriving = [], []
    for chunk in range(CHUNKS):
        span = slice(chunk * size, (chunk + 1) * size)
        held = [source_slab[:, span]]
        lane = chunk % LANES
        if ended[lane] is not None:
            held[0], _ = lax.optimization_barrier((held[0], ended[lane]))
        for _ in range(rows - 1):
            held.append(lax.ppermute(held[-1], "col", ring))
        ended[lane] = held[-1]
        blocks = []
        for j in range(rows):
            block = pick(held, ((row ^ j) - plane) % rows)
            blocks.append(block if j == 0 else lax.ppermute(block, "row", across[j]))
        mine = jnp.concatenate(blocks, axis=1)
        new_real, new_imag = 0.0, 0.0
        for q in range(share):
            portion = mine if q == 0 else lax.ppermute(mine, "col", inner[q])
            side_real, side_imag = sides[q]
            new_real += contract(portion[0], side_real) - contract(portion[1], side_imag)
            new_imag += contract(portion[0], side_imag) + contract(portion[1], side_real)
        partial = jnp.stack([new_real, new_imag])
        partials.append(partial)
        arriving.append(
            [
                lax.ppermute(partial[:, j * size : (j + 1) * size], "row", across[j])
                for j in range(1, rows)
            ]
        )
    for chunk in range(CHUNKS):
        span = slice(chunk * size, (chunk + 1) * size)
        received = lax.optimization_barrier((*arriving[chunk], partials[-1]))[: rows - 1]
        total = sum(received, partials[chunk][:, :size])
        here = mapped[:, span]
        primary_real = recorded[0, span] - (here[0] * total[0] - here[1] * total[1])
        primary_imag = recorded[1, span] - (here[0] * total[1] + here[1] * total[0])
        all_multiples.append(total)
        all_primaries.append(jnp.stack([primary_real, primary_imag]))
    return (jnp.concatenate(all_multiples, axis=1), jnp.concatenate(all_primaries, axis=1))


def solution(mesh):
    placed = (
        P(None, "row", "col"),
        P(None, "col", "row"),
        P(None, "row"),
        P(None, "row", "col"),
        P(None, ("row", "col")),
        P("row"),
        P("col"),
    )
    return jax.shard_map(
        local,
        mesh=mesh,
        in_specs=placed,
        out_specs=(P(None, "row", "col"), P(None, "row", "col")),
        check_vma=False,
    )
```

```python
import jax
import jax.numpy as jnp
from jax import lax
from jax.sharding import PartitionSpec as P

PHASE_STEP = 0.37
PRECISE = lax.Precision.HIGHEST
CHUNKS = 4
LANES = 2


def contract(left_side, right_side):
    return lax.dot_general(
        left_side,
        right_side,
        (((1,), (1,)), ((), ())),
        precision=lax.Precision.HIGH,
        preferred_element_type=jnp.float32,
    )


def weighted(receiver_side, surface_weight):
    weight_real = (
        receiver_side[0] * surface_weight[0][None, :]
        - receiver_side[1] * surface_weight[1][None, :]
    )
    weight_imag = (
        receiver_side[0] * surface_weight[1][None, :]
        + receiver_side[1] * surface_weight[0][None, :]
    )
    return (weight_real, weight_imag)


def responses(matching_taps):
    center = (matching_taps.shape[0] - 1) / 2.0
    phases = PHASE_STEP * (jnp.arange(matching_taps.shape[0], dtype=jnp.float32) - center)
    phase_table = jnp.stack([jnp.cos(phases), -jnp.sin(phases)])
    return jnp.dot(
        phase_table, matching_taps, precision=PRECISE, preferred_element_type=jnp.float32
    )


def applied_response(matching_taps, source_group, receiver_window, rows):
    response = responses(matching_taps)
    own = response.shape[1]
    cols = lax.axis_size("col")
    place = (lax.axis_index("row") * cols + lax.axis_index("col")) * own
    response = lax.dynamic_update_slice_in_dim(
        jnp.zeros((2, rows * cols * own), jnp.float32), response, place, axis=1
    )
    for axis, extent in (("col", cols), ("row", rows)):
        step = 1
        while step < extent:
            swap = [(i, i ^ step) for i in range(extent)]
            response = response + lax.ppermute(response, axis, swap)
            step *= 2
    groups = 4 * rows
    windows = response.shape[1] // groups
    response_grid = response.reshape(2, windows, groups)
    group_hot = (source_group[:, None] == jnp.arange(groups, dtype=jnp.int32)[None, :]).astype(
        jnp.float32
    )
    window_hot = (receiver_window[:, None] == jnp.arange(windows, dtype=jnp.int32)[None, :]).astype(
        jnp.float32
    )
    per_source = jnp.einsum("sg,cwg->csw", group_hot, response_grid, precision=PRECISE)
    return jnp.einsum("csw,rw->csr", per_source, window_hot, precision=PRECISE)


def pick(held, which):
    chosen = held[0]
    for number in range(1, len(held)):
        chosen = jnp.where(which == number, held[number], chosen)
    return chosen


def local(
    source_slab,
    receiver_side,
    surface_weight,
    recorded,
    matching_taps,
    source_group,
    receiver_window,
):
    rows, cols = lax.axis_size("row"), lax.axis_size("col")
    share = cols // rows
    row, col = lax.axis_index("row"), lax.axis_index("col")
    plane, part = col // share, col % share
    sources, depth = source_slab.shape[1], source_slab.shape[2]
    ring = [(c, (c - share) % cols) for c in range(cols)]
    across = [[(i, i ^ j) for i in range(rows)] for j in range(rows)]
    inner = [
        [(c, c // share * share + (c - q) % share) for c in range(cols)] for q in range(share)
    ]

    weight_real, weight_imag = weighted(receiver_side, surface_weight)
    sides = []
    for q in range(share):
        start = (part + q) % share * depth
        sides.append(
            (
                lax.dynamic_slice_in_dim(weight_real, start, depth, axis=1),
                lax.dynamic_slice_in_dim(weight_imag, start, depth, axis=1),
            )
        )
    mapped = applied_response(matching_taps, source_group, receiver_window, rows)

    size = sources // CHUNKS
    all_multiples, all_primaries = [], []
    ended = [None] * LANES
    partials, arriving = [], []
    for chunk in range(CHUNKS):
        span = slice(chunk * size, (chunk + 1) * size)
        held = [source_slab[:, span]]
        lane = chunk % LANES
        if ended[lane] is not None:
            held[0], _ = lax.optimization_barrier((held[0], ended[lane]))
        for _ in range(rows - 1):
            held.append(lax.ppermute(held[-1], "col", ring))
        ended[lane] = held[-1]
        if chunk == CHUNKS - 1:
            held[0] = lax.optimization_barrier((held[0], partials[0]))[0]
        blocks = []
        for j in range(rows):
            block = pick(held, ((row ^ j) - plane) % rows)
            blocks.append(block if j == 0 else lax.ppermute(block, "row", across[j]))
        mine = jnp.concatenate(blocks, axis=1)
        new_real, new_imag = 0.0, 0.0
        for q in range(share):
            portion = mine if q == 0 else lax.ppermute(mine, "col", inner[q])
            side_real, side_imag = sides[q]
            new_real += contract(portion[0], side_real) - contract(portion[1], side_imag)
            new_imag += contract(portion[0], side_imag) + contract(portion[1], side_real)
        partial = jnp.stack([new_real, new_imag])
        partials.append(partial)
        arriving.append(
            [
                lax.ppermute(partial[:, j * size : (j + 1) * size], "row", across[j])
                for j in range(1, rows)
            ]
        )
    for chunk in range(CHUNKS):
        span = slice(chunk * size, (chunk + 1) * size)
        received = lax.optimization_barrier((*arriving[chunk], partials[-1]))[: rows - 1]
        total = sum(received, partials[chunk][:, :size])
        here = mapped[:, span]
        primary_real = recorded[0, span] - (here[0] * total[0] - here[1] * total[1])
        primary_imag = recorded[1, span] - (here[0] * total[1] + here[1] * total[0])
        all_multiples.append(total)
        all_primaries.append(jnp.stack([primary_real, primary_imag]))
    return (jnp.concatenate(all_multiples, axis=1), jnp.concatenate(all_primaries, axis=1))


def solution(mesh):
    placed = (
        P(None, "row", "col"),
        P(None, "col", "row"),
        P(None, "row"),
        P(None, "row", "col"),
        P(None, ("row", "col")),
        P("row"),
        P("col"),
    )
    return jax.shard_map(
        local,
        mesh=mesh,
        in_specs=placed,
        out_specs=(P(None, "row", "col"), P(None, "row", "col")),
        check_vma=False,
    )
```
